512 devices in a mesh: seq: 16 (over x, z_hi), kvh: 8 (over y, core), rep: 4 (over z_lo).
Axes of the slice: x: 4, y: 4, z: 16 (z_hi: 4, z_lo: 4; z = z_hi * 4 + z_lo), core: 2. Of those that a mesh axis runs over, the one named last changes fastest.
Arguments:
- queries: bfloat16 [32, 8, 16, 128], P('rep', 'kvh'), parts along dimension 0, may hold values from -6 to 6
- slot_key_cache: bfloat16 [32, 8, 4096, 128], P('rep', 'kvh', 'seq'), parts along dimension 0, may hold values from -6 to 6
- slot_value_cache: bfloat16 [32, 8, 4096, 128], P('rep', 'kvh', 'seq'), parts along dimension 0, may hold values from -24 to 24
- lengths: int32 [32], P('rep'), parts along dimension 0, may hold values from 512 to 4096, as said below
- output_weight_matrix: bfloat16 [8, 16, 128, 8192], P('kvh', 'seq'), may hold values from -0.125 to 0.125
- residual: float32 [32, 8192], P('rep', ('seq', 'kvh')), parts along dimension 0, may hold values from -6 to 6
Outputs:
- hidden_out: float32 [32, 8192], P('rep', ('seq', 'kvh')), parts along dimension 0
The draws below stay inside these ranges and needn't reach their ends.
There are 4 independent parts, one for each index of `rep`. The reference program is written for one: setup_inputs(seed, part) draws one part's arguments, and reference() takes and returns one part's arrays. A program takes and returns all parts, laid end to end along the dimension named above; an argument that names none is the same for every part. Nothing has to cross between parts.
Inputs may be any that keep to these rules, and one draw needn't show every extreme that they name: Some row has 4096 live positions and some row 512; a row's live block count is lengths rounded up to whole blocks of 32.
All inputs are finite; a program needn't handle non-finite values.
Results may differ from the reference program's by a relative error of at most 0.0028.
Values sent between devices are 32-bit elements; how exact they have to be, the bound alone decides.
No kernel may reach another device: no remote copies, remote signals or barrier semaphores. Data moves between devices by JAX's collectives and lax.ppermute only.
A program may use at most 64 MiB of HBM per device.

```python
import math
import jax
import jax.numpy as jnp
from jax import lax

HEAD_DIMENSION = 128
OUTPUT_FEATURES = 8192
DECODE_ROWS = 8
SHARD_SLOTS = 256
BLOCK_POSITIONS = 32
CACHE_SHARDS = 16
QUERY_PER_KEY = 16
KEY_HEADS = 8
CONTEXT_SLOTS = 4096
SHORTEST = 512


def draw_slot_key_cache(key, part):
    random_root_key = jax.random.fold_in(key, 11)
    value_vectors = jax.random.normal(random_root_key, (DECODE_ROWS, KEY_HEADS, CONTEXT_SLOTS, HEAD_DIMENSION), jnp.float32)
    return jnp.clip(value_vectors, -6.0, 6.0).astype(jnp.bfloat16)


def draw_queries(key, part):
    random_root_key = jax.random.fold_in(key, 13)
    value_vectors = jax.random.normal(random_root_key, (DECODE_ROWS, KEY_HEADS, QUERY_PER_KEY, HEAD_DIMENSION), jnp.float32)
    return jnp.clip(value_vectors, -6.0, 6.0).astype(jnp.bfloat16)


def draw_lengths(key, part):
    drawn = jax.random.randint(jax.random.fold_in(key, 3), (DECODE_ROWS,), SHORTEST, CONTEXT_SLOTS + 1)
    ordering = jax.random.permutation(jax.random.fold_in(key, 5), DECODE_ROWS)
    drawn = drawn.at[ordering[0]].set(CONTEXT_SLOTS)
    drawn = drawn.at[ordering[1]].set(SHORTEST)
    return drawn.astype(jnp.int32)


def block_scale(stream_key, extent, cuts, low, largest):
    gain = 1.0
    for dim, parts in cuts:
        steps = jax.random.uniform(jax.random.fold_in(jax.random.fold_in(stream_key, 6), dim), (parts,), jnp.float32, low / len(cuts), largest / len(cuts))
        gain = gain * jnp.repeat(jnp.exp(steps), extent[dim] // parts).reshape((-1,) + (1,) * (len(extent) - 1 - dim))
    return gain


def bell_draw(stream_key, dims, deviation, reach, pieces=(), held_as=jnp.bfloat16):
    level = block_scale(stream_key, dims, pieces, -0.22, 0.18) if pieces else 1.0
    array = jax.random.normal(stream_key, dims, jnp.float32) * deviation * level
    return jnp.minimum(jnp.maximum(array, -reach), reach).astype(held_as)


def setup_inputs(seed: int = 0, part: int = 0) -> dict:
    key_of = jax.random.split(jax.random.key(seed), 7)
    own_keys = jax.random.split(jax.random.fold_in(key_of[6], part), 7)
    queries = draw_queries(jax.random.fold_in(jax.random.fold_in(key_of[6], part), 71), part)
    slot_key_cache = draw_slot_key_cache(jax.random.fold_in(jax.random.fold_in(key_of[6], part), 71), part)
    slot_value_cache = bell_draw(own_keys[2], (DECODE_ROWS, KEY_HEADS, CONTEXT_SLOTS, HEAD_DIMENSION), 4.0, 24.0, ((1, 8), (2, 16)))
    lengths = draw_lengths(jax.random.fold_in(jax.random.fold_in(key_of[6], part), 71), part)
    output_weight_matrix = bell_draw(key_of[4], (KEY_HEADS, QUERY_PER_KEY, HEAD_DIMENSION, OUTPUT_FEATURES), (QUERY_PER_KEY * HEAD_DIMENSION) ** -0.5, 0.125, ((0, 8), (1, 16)))
    residual = bell_draw(own_keys[5], (DECODE_ROWS, OUTPUT_FEATURES), 1.0, 6.0, ((1, 128),), jnp.float32)
    return dict(queries=queries, slot_key_cache=slot_key_cache, slot_value_cache=slot_value_cache, lengths=lengths, output_weight_matrix=output_weight_matrix, residual=residual)


def reference(queries, slot_key_cache, slot_value_cache, lengths, output_weight_matrix, residual):
    scale = 1.0 / math.sqrt(HEAD_DIMENSION)
    gathered_keys = slot_key_cache.astype(jnp.float32).reshape(DECODE_ROWS, KEY_HEADS, CACHE_SHARDS, SHARD_SLOTS, HEAD_DIMENSION)
    gathered_values = slot_value_cache.astype(jnp.float32).reshape(DECODE_ROWS, KEY_HEADS, CACHE_SHARDS, SHARD_SLOTS, HEAD_DIMENSION)
    slot_local = jnp.arange(SHARD_SLOTS, dtype=jnp.int32)
    shard_ids = jnp.arange(CACHE_SHARDS, dtype=jnp.int32)
    positions = (slot_local[None, :] // BLOCK_POSITIONS * CACHE_SHARDS + shard_ids[:, None]) * BLOCK_POSITIONS + slot_local[None, :] % BLOCK_POSITIONS
    visible = positions[None, :, :] < lengths.astype(jnp.int32)[:, None, None]
    scores = jnp.einsum('bkgd,bkscd->bkgsc', queries.astype(jnp.float32), gathered_keys) * scale
    scores = jnp.where(visible[:, None, None, :, :], scores, -1e+30)
    maximum = lax.optimization_barrier(jnp.max(scores, axis=-1))
    weights = jnp.exp(scores - maximum[..., None])
    totals = lax.optimization_barrier(jnp.sum(weights, axis=-1))
    rounded = lax.optimization_barrier(weights.astype(jnp.bfloat16)).astype(jnp.float32)
    summed = jnp.einsum('bkgsc,bkscd->bkgsd', rounded, gathered_values)
    partial_value = summed / totals[..., None]
    log_sums = maximum + jnp.log(totals)
    highest = lax.optimization_barrier(jnp.max(log_sums, axis=3))
    factors = jnp.exp(log_sums - highest[..., None])
    attention_output = lax.optimization_barrier(jnp.sum(factors[..., None] * partial_value, axis=3)) / lax.optimization_barrier(jnp.sum(factors, axis=3))[..., None]
    flattened_attention = attention_output.astype(jnp.bfloat16).reshape(DECODE_ROWS, KEY_HEADS * QUERY_PER_KEY * HEAD_DIMENSION)
    projected_output = jnp.dot(flattened_attention, output_weight_matrix.reshape(KEY_HEADS * QUERY_PER_KEY * HEAD_DIMENSION, OUTPUT_FEATURES), preferred_element_type=jnp.float32)
    return residual + projected_output
```

```python
import math

import jax
import jax.numpy as jnp
from jax import lax
from jax.sharding import PartitionSpec as P

BLOCK_POSITIONS = 32


def body(queries, slot_key_cache, slot_value_cache, lengths, output_weight_matrix, residual):
    shard_count = lax.axis_size("seq")
    shard_index = lax.axis_index("seq")
    group_query = queries[:, 0]
    key_rows = slot_key_cache[:, 0]
    value_rows = slot_value_cache[:, 0]
    slot_count = key_rows.shape[1]
    head_size = key_rows.shape[2]
    scale = 1.0 / math.sqrt(head_size)
    slot_ids = jnp.arange(slot_count, dtype=jnp.int32)
    positions = (
        slot_ids // BLOCK_POSITIONS * shard_count + shard_index
    ) * BLOCK_POSITIONS + slot_ids % BLOCK_POSITIONS
    visible = positions[None, :] < lengths[:, None]
    scores = (
        jnp.einsum("bgd,bcd->gbc", group_query, key_rows, preferred_element_type=jnp.float32)
        * scale
    )
    scores = jnp.where(visible[None], scores, -1e30)
    maximum = jnp.max(scores, axis=2)
    weights = jnp.exp(scores - maximum[..., None])
    totals = jnp.sum(weights, axis=2)
    rounded = weights.astype(jnp.bfloat16)
    summed = jnp.einsum("gbc,bcd->gbd", rounded, value_rows, preferred_element_type=jnp.float32)
    partial_value = summed / totals[..., None]
    log_sums = jnp.broadcast_to((maximum + jnp.log(totals))[..., None], partial_value.shape)
    sent = jnp.concatenate([partial_value, log_sums], axis=1)
    got = lax.all_to_all(sent, "seq", 0, 0, tiled=True)
    rows = partial_value.shape[1]
    logs = got[:, rows:]
    factors = jnp.exp(logs - jnp.max(logs, axis=0))
    attention_output = jnp.sum(factors * got[:, :rows], axis=0) / jnp.sum(factors, axis=0)
    out_rows = output_weight_matrix[0, 0]
    contrib = jnp.dot(
        attention_output.astype(jnp.bfloat16), out_rows, preferred_element_type=jnp.float32
    )
    width = residual.shape[1]
    pieces = contrib.reshape(rows, -1, width).transpose(1, 0, 2)
    exchanged = lax.all_to_all(pieces, ("seq", "kvh"), 0, 0, tiled=True)
    return residual + jnp.sum(exchanged, axis=0)


def solution(mesh):
    in_specs = (
        P("rep", "kvh", None, None),
        P("rep", "kvh", "seq", None),
        P("rep", "kvh", "seq", None),
        P("rep"),
        P("kvh", "seq", None, None),
        P("rep", ("seq", "kvh")),
    )
    out_specs = P("rep", ("seq", "kvh"))
    return jax.shard_map(body, mesh=mesh, in_specs=in_specs, out_specs=out_specs, check_vma=False)
```

```python
import math

import jax
import jax.numpy as jnp
from jax import lax
from jax.experimental import pallas as pl
from jax.experimental.pallas import tpu as pltpu
from jax.sharding import Mesh, PartitionSpec as P

BLOCK_POSITIONS = 32
LANES = 128
MEBI = 1 << 20
SEQ = ("x", "z_hi")
KVH = ("y", "core")


def attend_kernel(shards, lengths_ref, query_hbm, key_hbm, value_hbm, matrix_hbm,
                  sent_ref, matrix_ref, query_ref, key_ref, value_ref, query_sem, key_sem, value_sem, matrix_sem):
    rows, groups, size = query_ref.shape
    slots = key_ref.shape[1]
    query_copy = pltpu.make_async_copy(query_hbm, query_ref, query_sem)
    key_copies = [pltpu.make_async_copy(key_hbm.at[b], key_ref.at[b], key_sem.at[b]) for b in range(rows)]
    value_copies = [
        pltpu.make_async_copy(value_hbm.at[b], value_ref.at[b], value_sem.at[b]) for b in range(rows)
    ]
    matrix_copy = pltpu.make_async_copy(matrix_hbm, matrix_ref, matrix_sem)
    query_copy.start()
    for copy in key_copies:
        copy.start()
    for copy in value_copies:
        copy.start()
    matrix_copy.start()
    scale = 1.0 / math.sqrt(size)
    slot_ids = lax.broadcasted_iota(jnp.int32, (groups, slots), 1)
    positions = (
        slot_ids // BLOCK_POSITIONS * shards + lax.axis_index(SEQ)
    ) * BLOCK_POSITIONS + slot_ids % BLOCK_POSITIONS
    query_copy.wait()
    scores = []
    for b in range(rows):
        key_copies[b].wait()
        scores.append(
            lax.dot_general(
                query_ref[b], key_ref[b], (((1,), (1,)), ((), ())), preferred_element_type=jnp.float32
            )
        )
    logs = jnp.zeros((groups, LANES), jnp.float32)
    lane = lax.broadcasted_iota(jnp.int32, (groups, LANES), 1)
    weights = []
    totals = []
    for b in range(rows):
        masked = jnp.where(positions < lengths_ref[b], scores[b] * scale, -1e30)
        top = jnp.max(masked, axis=1, keepdims=True)
        weight = jnp.exp(masked - top)
        total = jnp.sum(weight, axis=1, keepdims=True)
        weights.append(weight.astype(jnp.bfloat16))
        totals.append(total)
        logs = jnp.where(lane == b, top + jnp.log(total), logs)
    for b in range(rows):
        value_copies[b].wait()
        summed = jnp.dot(weights[b], value_ref[b], preferred_element_type=jnp.float32)
        sent_ref[pl.ds(b, groups, stride=rows + 1), :] = summed / totals[b]
    sent_ref[pl.ds(rows, groups, stride=rows + 1), :] = logs
    matrix_copy.wait()


def attend(lengths, queries, keys, values, matrix, shards):
    rows, groups, size = queries.shape
    slots = keys.shape[1]
    outside = pl.BlockSpec(memory_space=pltpu.HBM)
    inside = pl.BlockSpec(memory_space=pltpu.VMEM)
    scalars = pl.BlockSpec(memory_space=pltpu.SMEM)
    return pl.pallas_call(
        lambda *refs: attend_kernel(shards, *refs),
        name="attend",
        compiler_params=pltpu.CompilerParams(vmem_limit_bytes=8 * MEBI),
        out_shape=(
            jax.ShapeDtypeStruct((groups * (rows + 1), size), jnp.float32),
            jax.ShapeDtypeStruct(matrix.shape, matrix.dtype),
        ),
        in_specs=[scalars, outside, outside, outside, outside],
        out_specs=(inside, inside),
        scratch_shapes=[
            pltpu.VMEM((rows, groups, size), queries.dtype),
            pltpu.VMEM((rows, slots, size), keys.dtype),
            pltpu.VMEM((rows, slots, size), values.dtype),
            pltpu.SemaphoreType.DMA,
            pltpu.SemaphoreType.DMA((rows,)),
            pltpu.SemaphoreType.DMA((rows,)),
            pltpu.SemaphoreType.DMA,
        ],
    )(*[pltpu.with_memory_space_constraint(a, pltpu.HBM) for a in (lengths, queries, keys, values, matrix)])


def project_kernel(order, got_ref, weight_ref, out_ref):
    pieces, rows, lanes = out_ref.shape
    shards = got_ref.shape[0] // (rows + 1)
    logs = got_ref[pl.ds(rows, shards, stride=rows + 1), :]
    factors = jnp.exp(logs - jnp.max(logs, axis=0, keepdims=True))
    factors = factors / jnp.sum(factors, axis=0, keepdims=True)
    diagonal = lax.broadcasted_iota(jnp.int32, (rows, lanes), 0) == lax.broadcasted_iota(
        jnp.int32, (rows, lanes), 1
    )
    attended = jnp.zeros((rows, lanes), jnp.float32)
    for s in range(shards):
        factor = jnp.sum(
            jnp.where(diagonal, factors[s : s + 1, :], 0.0), axis=1, keepdims=True
        )
        attended += factor * got_ref[pl.ds(s * (rows + 1), rows), :]
    attended = attended.astype(jnp.bfloat16)
    step = 8
    for first in range(0, pieces, step):
        product = jnp.dot(
            attended,
            weight_ref[:, first * lanes : (first + step) * lanes],
            preferred_element_type=jnp.float32,
        )
        for j in range(step):
            out_ref[order[first + j]] = product[:, j * lanes : (j + 1) * lanes]


def project(got, weights, order, rows):
    size, features = weights.shape
    return pl.pallas_call(
        lambda *refs: project_kernel(order, *refs),
        name="project",
        compiler_params=pltpu.CompilerParams(vmem_limit_bytes=8 * MEBI),
        out_shape=jax.ShapeDtypeStruct((features // LANES, rows, LANES), jnp.float32),
        in_specs=[pl.BlockSpec(memory_space=pltpu.VMEM)] * 2,
        out_specs=pl.BlockSpec(memory_space=pltpu.VMEM),
    )(got, weights)


def plane_sum_kernel(got_ref, out_ref):
    sources, blocks = got_ref.shape[:2]
    copies = out_ref.shape[0] // blocks
    for i in range(blocks):
        total = got_ref[0, i]
        for s in range(1, sources):
            total += got_ref[s, i]
        for c in range(copies):
            out_ref[i * copies + c] = total


def plane_sum(got, blocks, copies):
    pieces, rows, lanes = got.shape
    return pl.pallas_call(
        plane_sum_kernel,
        name="plane_sum",
        compiler_params=pltpu.CompilerParams(vmem_limit_bytes=2 * MEBI),
        out_shape=jax.ShapeDtypeStruct((blocks * copies, rows, lanes), jnp.float32),
        in_specs=[pl.BlockSpec(memory_space=pltpu.VMEM)],
        out_specs=pl.BlockSpec(memory_space=pltpu.VMEM),
    )(got.reshape(pieces // blocks, blocks, rows, lanes))


def finish_kernel(got_ref, residual_ref, out_ref):
    width = out_ref.shape[1]
    total = got_ref[0]
    for s in range(1, got_ref.shape[0]):
        total += got_ref[s]
    half = jnp.where(lax.axis_index("core") == 0, total[:, :width], total[:, width:])
    out_ref[...] = residual_ref[...] + half


def finish(got, residual):
    return pl.pallas_call(
        finish_kernel,
        name="finish",
        compiler_params=pltpu.CompilerParams(vmem_limit_bytes=2 * MEBI),
        out_shape=jax.ShapeDtypeStruct(residual.shape, jnp.float32),
        in_specs=[pl.BlockSpec(memory_space=pltpu.VMEM)] * 2,
        out_specs=pl.BlockSpec(memory_space=pltpu.VMEM),
    )(got, residual)


def body(queries, slot_key_cache, slot_value_cache, lengths, output_weight_matrix, residual):
    x_size, z_size = lax.axis_size("x"), lax.axis_size("z_hi")
    y_size, cores = lax.axis_size("y"), lax.axis_size("core")
    shards = x_size * z_size
    rows = queries.shape[0]
    sent, matrix = attend(
        lengths,
        queries[:, 0],
        slot_key_cache[:, 0],
        slot_value_cache[:, 0],
        output_weight_matrix[0, 0],
        shards,
    )
    lines, size = sent.shape
    got = lax.all_to_all(sent.reshape(lines, 1, size), SEQ, 0, 0, tiled=True).reshape(lines, size)
    order = [
        (x * y_size + y) * z_size + z
        for x in range(x_size)
        for z in range(z_size)
        for y in range(y_size)
    ]
    pieces = project(got, matrix, order, rows)
    plane = lax.all_to_all(pieces, ("x", "y"), 0, 0, tiled=True)
    blocks = plane_sum(plane, z_size, cores)
    last = lax.all_to_all(blocks, ("z_hi", "core"), 0, 0, tiled=True)
    return finish(last, residual)


def solution(mesh):
    fine = Mesh(
        mesh.devices.reshape(4, mesh.shape["seq"] // 4, mesh.shape["kvh"] // 2, 2, mesh.shape["rep"]),
        ("x", "z_hi", "y", "core", "rep"),
    )
    in_specs = (
        P("rep", KVH, None, None),
        P("rep", KVH, SEQ, None),
        P("rep", KVH, SEQ, None),
        P("rep"),
        P(KVH, SEQ, None, None),
        P("rep", SEQ + KVH),
    )
    out_specs = P("rep", SEQ + KVH)
    return jax.shard_map(body, mesh=fine, in_specs=in_specs, out_specs=out_specs, check_vma=False)
```

```python
import math

import jax
import jax.numpy as jnp
from jax import lax
from jax.experimental import pallas as pl
from jax.experimental.pallas import tpu as pltpu
from jax.sharding import Mesh, PartitionSpec as P

BLOCK_POSITIONS = 32
LANES = 128
MEBI = 1 << 20
SEQ = ("x", "z_hi")
KVH = ("y", "core")


def attend_kernel(shards, lengths_hbm, query_hbm, key_hbm, value_hbm, matrix_hbm, sent_ref, matrix_ref,
                  lengths_ref, query_ref, key_ref, value_ref, sems):
    rows, groups, size = query_ref.shape
    slots = key_ref.shape[1]
    lengths_copy, query_copy, key_copy, value_copy, matrix_copy = [
        pltpu.make_async_copy(source, target, sems.at[i])
        for i, (source, target) in enumerate(
            (
                (lengths_hbm, lengths_ref),
                (query_hbm, query_ref),
                (key_hbm, key_ref),
                (value_hbm, value_ref),
                (matrix_hbm, matrix_ref),
            )
        )
    ]
    lengths_copy.start()
    query_copy.start()
    key_copy.start()
    value_copy.start()
    matrix_copy.start()
    scale = 1.0 / math.sqrt(size)
    slot_ids = lax.broadcasted_iota(jnp.int32, (groups, slots), 1)
    positions = (
        slot_ids // BLOCK_POSITIONS * shards + lax.axis_index(SEQ)
    ) * BLOCK_POSITIONS + slot_ids % BLOCK_POSITIONS
    lane = lax.broadcasted_iota(jnp.int32, (groups, LANES), 1)
    lengths_copy.wait()
    query_copy.wait()
    key_copy.wait()
    scores = [
        lax.dot_general(
            query_ref[b], key_ref[b], (((1,), (1,)), ((), ())), preferred_element_type=jnp.float32
        )
        for b in range(rows)
    ]
    logs = jnp.zeros((groups, LANES), jnp.float32)
    weights = []
    totals = []
    for b in range(rows):
        masked = jnp.where(positions < lengths_ref[b], scores[b] * scale, -1e30)
        top = jnp.max(masked, axis=1, keepdims=True)
        weight = jnp.exp(masked - top)
        total = jnp.sum(weight, axis=1, keepdims=True)
        weights.append(weight.astype(jnp.bfloat16))
        totals.append(total)
        logs = jnp.where(lane == b, top + jnp.log(total), logs)
    value_copy.wait()
    for b in range(rows):
        summed = jnp.dot(weights[b], value_ref[b], preferred_element_type=jnp.float32)
        sent_ref[pl.ds(b, groups, stride=rows + 1), :] = summed / totals[b]
    sent_ref[pl.ds(rows, groups, stride=rows + 1), :] = logs
    matrix_copy.wait()


def attend(lengths, queries, keys, values, matrix, shards):
    rows, groups, size = queries.shape
    outside = pl.BlockSpec(memory_space=pltpu.HBM)
    inside = pl.BlockSpec(memory_space=pltpu.VMEM)
    operands = (lengths, queries, keys, values, matrix)
    return pl.pallas_call(
        lambda *refs: attend_kernel(shards, *refs),
        name="attend",
        compiler_params=pltpu.CompilerParams(vmem_limit_bytes=8 * MEBI),
        out_shape=(
            jax.ShapeDtypeStruct((groups * (rows + 1), size), jnp.float32),
            jax.ShapeDtypeStruct(matrix.shape, matrix.dtype),
        ),
        in_specs=[outside] * len(operands),
        out_specs=(inside, inside),
        scratch_shapes=[pltpu.SMEM(lengths.shape, lengths.dtype)]
        + [pltpu.VMEM(a.shape, a.dtype) for a in (queries, keys, values)]
        + [pltpu.SemaphoreType.DMA((len(operands),))],
    )(*[pltpu.with_memory_space_constraint(a, pltpu.HBM) for a in operands])


def project_kernel(got_ref, weight_ref, out_ref):
    pieces, rows, lanes = out_ref.shape
    shards = got_ref.shape[0] // (rows + 1)
    logs = got_ref[pl.ds(rows, shards, stride=rows + 1), :]
    factors = jnp.exp(logs - jnp.max(logs, axis=0, keepdims=True))
    factors = factors / jnp.sum(factors, axis=0, keepdims=True)
    diagonal = lax.broadcasted_iota(jnp.int32, (rows, lanes), 0) == lax.broadcasted_iota(
        jnp.int32, (rows, lanes), 1
    )
    attended = jnp.zeros((rows, lanes), jnp.float32)
    for s in range(shards):
        factor = jnp.sum(
            jnp.where(diagonal, factors[s : s + 1, :], 0.0), axis=1, keepdims=True
        )
        attended += factor * got_ref[pl.ds(s * (rows + 1), rows), :]
    attended = attended.astype(jnp.bfloat16)
    step = 8
    for first in range(0, pieces, step):
        product = jnp.dot(
            attended,
            weight_ref[:, first * lanes : (first + step) * lanes],
            preferred_element_type=jnp.float32,
        )
        for j in range(step):
            out_ref[first + j] = product[:, j * lanes : (j + 1) * lanes]


def project(got, weights, rows):
    size, features = weights.shape
    return pl.pallas_call(
        project_kernel,
        name="project",
        compiler_params=pltpu.CompilerParams(vmem_limit_bytes=8 * MEBI),
        out_shape=jax.ShapeDtypeStruct((features // LANES, rows, LANES), jnp.float32),
        in_specs=[pl.BlockSpec(memory_space=pltpu.VMEM)] * 2,
        out_specs=pl.BlockSpec(memory_space=pltpu.VMEM),
    )(got, weights)


def core_sum_kernel(got_ref, out_ref):
    pieces, part, lanes = out_ref.shape
    half = lanes // 2
    low = lax.broadcasted_iota(jnp.int32, (part, lanes), 1) < half
    first = lax.axis_index("core") == 0
    for i in range(pieces):
        total = got_ref[0, i] + got_ref[1, i]
        other = pltpu.roll(total, half, 1)
        one = jnp.where(first, total, other)
        two = jnp.where(first, other, total)
        out_ref[i] = jnp.where(low, one[:part], two[part:])


def core_sum(got):
    cores, pieces, rows, lanes = got.shape
    return pl.pallas_call(
        core_sum_kernel,
        name="core_sum",
        compiler_params=pltpu.CompilerParams(vmem_limit_bytes=2 * MEBI),
        out_shape=jax.ShapeDtypeStruct((pieces, rows // cores, lanes), jnp.float32),
        in_specs=[pl.BlockSpec(memory_space=pltpu.VMEM)],
        out_specs=pl.BlockSpec(memory_space=pltpu.VMEM),
    )(got)


def finish_kernel(got_ref, residual_ref, out_ref):
    width = out_ref.shape[1]
    part = got_ref.shape[1]
    totals = [got_ref[s] for s in range(got_ref.shape[0])]
    while len(totals) > 1:
        totals = [totals[i] + totals[i + 1] for i in range(0, len(totals), 2)]
    out_ref[:part] = residual_ref[:part] + totals[0][:, :width]
    out_ref[part:] = residual_ref[part:] + totals[0][:, width:]


def finish(got, residual):
    return pl.pallas_call(
        finish_kernel,
        name="finish",
        compiler_params=pltpu.CompilerParams(vmem_limit_bytes=2 * MEBI),
        out_shape=jax.ShapeDtypeStruct(residual.shape, jnp.float32),
        in_specs=[pl.BlockSpec(memory_space=pltpu.VMEM)] * 2,
        out_specs=pl.BlockSpec(memory_space=pltpu.VMEM),
    )(got, residual)


def body(queries, slot_key_cache, slot_value_cache, lengths, output_weight_matrix, residual):
    shards = lax.axis_size(SEQ)
    rows = queries.shape[0]
    sent, matrix = attend(
        lengths,
        queries[:, 0],
        slot_key_cache[:, 0],
        slot_value_cache[:, 0],
        output_weight_matrix[0, 0],
        shards,
    )
    lines, size = sent.shape
    got = lax.all_to_all(sent.reshape(lines, 1, size), SEQ, 0, 0, tiled=True).reshape(lines, size)
    pieces = project(got, matrix, rows)
    both = lax.all_gather(pieces, "core")
    packed = core_sum(both)
    last = lax.all_to_all(packed, ("x", "z_hi", "y"), 0, 0, tiled=True)
    return finish(last, residual)


def solution(mesh):
    fine = Mesh(
        mesh.devices.reshape(4, mesh.shape["seq"] // 4, mesh.shape["kvh"] // 2, 2, mesh.shape["rep"]),
        ("x", "z_hi", "y", "core", "rep"),
    )
    in_specs = (
        P("rep", KVH, None, None),
        P("rep", KVH, SEQ, None),
        P("rep", KVH, SEQ, None),
        P("rep"),
        P(KVH, SEQ, None, None),
        P("rep", SEQ + KVH),
    )
    out_specs = P("rep", SEQ + KVH)
    return jax.shard_map(body, mesh=fine, in_specs=in_specs, out_specs=out_specs, check_vma=False)
```

```python
import math

import jax
import jax.numpy as jnp
from jax import lax
from jax.experimental import pallas as pl
from jax.experimental.pallas import tpu as pltpu
from jax.sharding import Mesh, PartitionSpec as P

BLOCK_POSITIONS = 32
LANES = 128
MEBI = 1 << 20
SEQ = ("x", "z1", "z0")
PEERS = ("z0", "z1", "x", "y")
KVH = ("y", "core")


def attend_kernel(shards, lengths_hbm, query_hbm, key_hbm, value_hbm, matrix_hbm, sent_ref, matrix_ref,
                  lengths_ref, query_ref, key_ref, value_ref, sems):
    rows, groups, size = query_ref.shape
    slots = key_ref.shape[1]
    lengths_copy, query_copy, key_copy, value_copy, matrix_copy = [
        pltpu.make_async_copy(source, target, sems.at[i])
        for i, (source, target) in enumerate(
            (
                (lengths_hbm, lengths_ref),
                (query_hbm, query_ref),
                (key_hbm, key_ref),
                (value_hbm, value_ref),
                (matrix_hbm, matrix_ref),
            )
        )
    ]
    lengths_copy.start()
    query_copy.start()
    key_copy.start()
    value_copy.start()
    matrix_copy.start()
    scale = 1.0 / math.sqrt(size)
    slot_ids = lax.broadcasted_iota(jnp.int32, (groups, slots), 1)
    positions = (
        slot_ids // BLOCK_POSITIONS * shards + lax.axis_index(SEQ)
    ) * BLOCK_POSITIONS + slot_ids % BLOCK_POSITIONS
    lane = lax.broadcasted_iota(jnp.int32, (groups, LANES), 1)
    lengths_copy.wait()
    query_copy.wait()
    key_copy.wait()
    scores = [
        lax.dot_general(
            query_ref[b], key_ref[b], (((1,), (1,)), ((), ())), preferred_element_type=jnp.float32
        )
        for b in range(rows)
    ]
    logs = jnp.zeros((groups, LANES), jnp.float32)
    weights = []
    totals = []
    for b in range(rows):
        masked = jnp.where(positions < lengths_ref[b], scores[b] * scale, -1e30)
        top = jnp.max(masked, axis=1, keepdims=True)
        weight = jnp.exp(masked - top)
        total = jnp.sum(weight, axis=1, keepdims=True)
        weights.append(weight.astype(jnp.bfloat16))
        totals.append(total)
        logs = jnp.where(lane == b, top + jnp.log(total), logs)
    value_copy.wait()
    for b in range(rows):
        summed = jnp.dot(weights[b], value_ref[b], preferred_element_type=jnp.float32)
        sent_ref[pl.ds(b, groups, stride=rows + 1), :] = summed / totals[b]
    sent_ref[pl.ds(rows, groups, stride=rows + 1), :] = logs
    matrix_copy.wait()


def attend(lengths, queries, keys, values, matrix, shards):
    rows, groups, size = queries.shape
    outside = pl.BlockSpec(memory_space=pltpu.HBM)
    inside = pl.BlockSpec(memory_space=pltpu.VMEM)
    operands = (lengths, queries, keys, values, matrix)
    return pl.pallas_call(
        lambda *refs: attend_kernel(shards, *refs),
        name="attend",
        compiler_params=pltpu.CompilerParams(vmem_limit_bytes=8 * MEBI),
        out_shape=(
            jax.ShapeDtypeStruct((groups * (rows + 1), size), jnp.float32),
            jax.ShapeDtypeStruct(matrix.shape, matrix.dtype),
        ),
        in_specs=[outside] * len(operands),
        out_specs=(inside, inside),
        scratch_shapes=[pltpu.SMEM(lengths.shape, lengths.dtype)]
        + [pltpu.VMEM(a.shape, a.dtype) for a in (queries, keys, values)]
        + [pltpu.SemaphoreType.DMA((len(operands),))],
    )(*[pltpu.with_memory_space_constraint(a, pltpu.HBM) for a in operands])


def project_kernel(places, got_ref, weight_ref, out_ref):
    pieces, rows, lanes = out_ref.shape
    shards = got_ref.shape[0] // (rows + 1)
    logs = got_ref[pl.ds(rows, shards, stride=rows + 1), :]
    factors = jnp.exp(logs - jnp.max(logs, axis=0, keepdims=True))
    factors = factors / jnp.sum(factors, axis=0, keepdims=True)
    diagonal = lax.broadcasted_iota(jnp.int32, (rows, lanes), 0) == lax.broadcasted_iota(
        jnp.int32, (rows, lanes), 1
    )
    attended = jnp.zeros((rows, lanes), jnp.float32)
    for s in range(shards):
        factor = jnp.sum(
            jnp.where(diagonal, factors[s : s + 1, :], 0.0), axis=1, keepdims=True
        )
        attended += factor * got_ref[pl.ds(s * (rows + 1), rows), :]
    attended = attended.astype(jnp.bfloat16)
    step = 8
    for first in range(0, pieces, step):
        product = jnp.dot(
            attended,
            weight_ref[:, first * lanes : (first + step) * lanes],
            preferred_element_type=jnp.float32,
        )
        for j in range(step):
            out_ref[places[first + j]] = product[:, j * lanes : (j + 1) * lanes]


def project(got, weights, places, rows):
    size, features = weights.shape
    return pl.pallas_call(
        lambda *refs: project_kernel(places, *refs),
        name="project",
        compiler_params=pltpu.CompilerParams(vmem_limit_bytes=8 * MEBI),
        out_shape=jax.ShapeDtypeStruct((features // LANES, rows, LANES), jnp.float32),
        in_specs=[pl.BlockSpec(memory_space=pltpu.VMEM)] * 2,
        out_specs=pl.BlockSpec(memory_space=pltpu.VMEM),
    )(got, weights)


def core_sum_kernel(got_ref, out_ref):
    pieces, part, lanes = out_ref.shape
    half = lanes // 2
    low = lax.broadcasted_iota(jnp.int32, (part, lanes), 1) < half
    first = lax.axis_index("core") == 0
    for i in range(pieces):
        total = got_ref[0, i] + got_ref[1, i]
        other = pltpu.roll(total, half, 1)
        one = jnp.where(first, total, other)
        two = jnp.where(first, other, total)
        out_ref[i] = jnp.where(low, one[:part], two[part:])


def core_sum(got):
    cores, pieces, rows, lanes = got.shape
    return pl.pallas_call(
        core_sum_kernel,
        name="core_sum",
        compiler_params=pltpu.CompilerParams(vmem_limit_bytes=2 * MEBI),
        out_shape=jax.ShapeDtypeStruct((pieces, rows // cores, lanes), jnp.float32),
        in_specs=[pl.BlockSpec(memory_space=pltpu.VMEM)],
        out_specs=pl.BlockSpec(memory_space=pltpu.VMEM),
    )(got)


def finish_kernel(got_ref, residual_ref, out_ref):
    width = out_ref.shape[1]
    part = got_ref.shape[1]
    totals = [got_ref[s] for s in range(got_ref.shape[0])]
    while len(totals) > 1:
        totals = [totals[i] + totals[i + 1] for i in range(0, len(totals), 2)]
    out_ref[:part] = residual_ref[:part] + totals[0][:, :width]
    out_ref[part:] = residual_ref[part:] + totals[0][:, width:]


def finish(got, residual):
    return pl.pallas_call(
        finish_kernel,
        name="finish",
        compiler_params=pltpu.CompilerParams(vmem_limit_bytes=2 * MEBI),
        out_shape=jax.ShapeDtypeStruct(residual.shape, jnp.float32),
        in_specs=[pl.BlockSpec(memory_space=pltpu.VMEM)] * 2,
        out_specs=pl.BlockSpec(memory_space=pltpu.VMEM),
    )(got, residual)


def body(queries, slot_key_cache, slot_value_cache, lengths, output_weight_matrix, residual):
    shards = lax.axis_size(SEQ)
    rows = queries.shape[0]
    sent, matrix = attend(
        lengths,
        queries[:, 0],
        slot_key_cache[:, 0],
        slot_value_cache[:, 0],
        output_weight_matrix[0, 0],
        shards,
    )
    lines, size = sent.shape
    got = lax.all_to_all(sent.reshape(lines, 1, size), SEQ, 0, 0, tiled=True).reshape(lines, size)
    sizes = [lax.axis_size(axis) for axis in PEERS]
    places = [
        ((z0 * sizes[1] + z1) * sizes[2] + x) * sizes[3] + y
        for x in range(sizes[2])
        for z1 in range(sizes[1])
        for z0 in range(sizes[0])
        for y in range(sizes[3])
    ]
    pieces = project(got, matrix, places, rows)
    both = lax.all_gather(pieces, "core")
    packed = core_sum(both)
    last = lax.all_to_all(packed, PEERS, 0, 0, tiled=True)
    return finish(last, residual)


def solution(mesh):
    fine = Mesh(
        mesh.devices.reshape(4, 2, mesh.shape["seq"] // 8, mesh.shape["kvh"] // 2, 2, mesh.shape["rep"]),
        ("x", "z1", "z0", "y", "core", "rep"),
    )
    in_specs = (
        P("rep", KVH, None, None),
        P("rep", KVH, SEQ, None),
        P("rep", KVH, SEQ, None),
        P("rep"),
        P(KVH, SEQ, None, None),
        P("rep", SEQ + KVH),
    )
    out_specs = P("rep", SEQ + KVH)
    return jax.shard_map(body, mesh=fine, in_specs=in_specs, out_specs=out_specs, check_vma=False)
```

```python
import math

import jax
import jax.numpy as jnp
from jax import lax
from jax.experimental import pallas as pl
from jax.experimental.pallas import tpu as pltpu
from jax.sharding import Mesh, PartitionSpec as P

BLOCK_POSITIONS = 32
LANES = 128
MEBI = 1 << 20
SEQ = ("x", "z_hi")
KVH = ("y", "core")
MESH_AXES = ("x", "z_hi", "y", "core", "rep")


def peer_chips(x_size, z_size, y_size):
    order = (0, 1, 3, 2)
    planes = (0, 2, 1, 3)
    chips = [
        (order[2 * x1 + x0], planes[z], order[2 * y1 + y0])
        for z in range(4)
        for x1 in range(2)
        for y1 in range(2)
        for x0 in range(2)
        for y0 in range(2)
    ]
    assert (x_size, z_size, y_size) == (4, 4, 4)
    return chips


def attend_kernel(shards, lengths_hbm, query_hbm, key_hbm, value_hbm, matrix_hbm, sent_ref, matrix_ref,
                  lengths_ref, query_ref, key_ref, value_ref, sems):
    rows, groups, size = query_ref.shape
    slots = key_ref.shape[1]
    lengths_copy, query_copy, key_copy, value_copy, matrix_copy = [
        pltpu.make_async_copy(source, target, sems.at[i])
        for i, (source, target) in enumerate(
            (
                (lengths_hbm, lengths_ref),
                (query_hbm, query_ref),
                (key_hbm, key_ref),
                (value_hbm, value_ref),
                (matrix_hbm, matrix_ref),
            )
        )
    ]
    lengths_copy.start()
    query_copy.start()
    key_copy.start()
    value_copy.start()
    matrix_copy.start()
    scale = 1.0 / math.sqrt(size)
    slot_ids = lax.broadcasted_iota(jnp.int32, (groups, slots), 1)
    positions = (
        slot_ids // BLOCK_POSITIONS * shards + lax.axis_index(SEQ)
    ) * BLOCK_POSITIONS + slot_ids % BLOCK_POSITIONS
    lane = lax.broadcasted_iota(jnp.int32, (groups, LANES), 1)
    lengths_copy.wait()
    query_copy.wait()
    key_copy.wait()
    scores = [
        lax.dot_general(
            query_ref[b], key_ref[b], (((1,), (1,)), ((), ())), preferred_element_type=jnp.float32
        )
        for b in range(rows)
    ]
    logs = jnp.zeros((groups, LANES), jnp.float32)
    weights = []
    totals = []
    for b in range(rows):
        masked = jnp.where(positions < lengths_ref[b], scores[b] * scale, -1e30)
        top = jnp.max(masked, axis=1, keepdims=True)
        weight = jnp.exp(masked - top)
        total = jnp.sum(weight, axis=1, keepdims=True)
        weights.append(weight.astype(jnp.bfloat16))
        totals.append(total)
        logs = jnp.where(lane == b, top + jnp.log(total), logs)
    value_copy.wait()
    for b in range(rows):
        summed = jnp.dot(weights[b], value_ref[b], preferred_element_type=jnp.float32)
        sent_ref[pl.ds(b, groups, stride=rows + 1), :] = summed / totals[b]
    sent_ref[pl.ds(rows, groups, stride=rows + 1), :] = logs
    matrix_copy.wait()


def attend(lengths, queries, keys, values, matrix, shards):
    rows, groups, size = queries.shape
    outside = pl.BlockSpec(memory_space=pltpu.HBM)
    inside = pl.BlockSpec(memory_space=pltpu.VMEM)
    operands = (lengths, queries, keys, values, matrix)
    return pl.pallas_call(
        lambda *refs: attend_kernel(shards, *refs),
        name="attend",
        compiler_params=pltpu.CompilerParams(vmem_limit_bytes=8 * MEBI),
        out_shape=(
            jax.ShapeDtypeStruct((groups * (rows + 1), size), jnp.float32),
            jax.ShapeDtypeStruct(matrix.shape, matrix.dtype),
        ),
        in_specs=[outside] * len(operands),
        out_specs=(inside, inside),
        scratch_shapes=[pltpu.SMEM(lengths.shape, lengths.dtype)]
        + [pltpu.VMEM(a.shape, a.dtype) for a in (queries, keys, values)]
        + [pltpu.SemaphoreType.DMA((len(operands),))],
    )(*[pltpu.with_memory_space_constraint(a, pltpu.HBM) for a in operands])


def project_kernel(places, got_ref, weight_ref, out_ref):
    pieces, rows, lanes = out_ref.shape
    shards = got_ref.shape[0] // (rows + 1)
    logs = got_ref[pl.ds(rows, shards, stride=rows + 1), :]
    factors = jnp.exp(logs - jnp.max(logs, axis=0, keepdims=True))
    factors = factors / jnp.sum(factors, axis=0, keepdims=True)
    diagonal = lax.broadcasted_iota(jnp.int32, (rows, lanes), 0) == lax.broadcasted_iota(
        jnp.int32, (rows, lanes), 1
    )
    attended = jnp.zeros((rows, lanes), jnp.float32)
    for s in range(shards):
        factor = jnp.sum(
            jnp.where(diagonal, factors[s : s + 1, :], 0.0), axis=1, keepdims=True
        )
        attended += factor * got_ref[pl.ds(s * (rows + 1), rows), :]
    attended = attended.astype(jnp.bfloat16)
    step = 8
    for first in range(0, pieces, step):
        product = jnp.dot(
            attended,
            weight_ref[:, first * lanes : (first + step) * lanes],
            preferred_element_type=jnp.float32,
        )
        for j in range(step):
            out_ref[places[first + j]] = product[:, j * lanes : (j + 1) * lanes]


def project(got, weights, places, rows):
    size, features = weights.shape
    return pl.pallas_call(
        lambda *refs: project_kernel(places, *refs),
        name="project",
        compiler_params=pltpu.CompilerParams(vmem_limit_bytes=8 * MEBI),
        out_shape=jax.ShapeDtypeStruct((features // LANES, rows, LANES), jnp.float32),
        in_specs=[pl.BlockSpec(memory_space=pltpu.VMEM)] * 2,
        out_specs=pl.BlockSpec(memory_space=pltpu.VMEM),
    )(got, weights)


def core_sum_kernel(got_ref, out_ref):
    pieces, part, lanes = out_ref.shape
    half = lanes // 2
    low = lax.broadcasted_iota(jnp.int32, (part, lanes), 1) < half
    first = lax.axis_index("core") == 0
    for i in range(pieces):
        total = got_ref[0, i] + got_ref[1, i]
        other = pltpu.roll(total, half, 1)
        one = jnp.where(first, total, other)
        two = jnp.where(first, other, total)
        out_ref[i] = jnp.where(low, one[:part], two[part:])


def core_sum(got):
    cores, pieces, rows, lanes = got.shape
    return pl.pallas_call(
        core_sum_kernel,
        name="core_sum",
        compiler_params=pltpu.CompilerParams(vmem_limit_bytes=2 * MEBI),
        out_shape=jax.ShapeDtypeStruct((pieces, rows // cores, lanes), jnp.float32),
        in_specs=[pl.BlockSpec(memory_space=pltpu.VMEM)],
        out_specs=pl.BlockSpec(memory_space=pltpu.VMEM),
    )(got)


def finish_kernel(got_ref, residual_ref, out_ref):
    width = out_ref.shape[1]
    part = got_ref.shape[1]
    totals = [got_ref[s] for s in range(got_ref.shape[0])]
    while len(totals) > 1:
        totals = [totals[i] + totals[i + 1] for i in range(0, len(totals), 2)]
    out_ref[:part] = residual_ref[:part] + totals[0][:, :width]
    out_ref[part:] = residual_ref[part:] + totals[0][:, width:]


def finish(got, residual):
    return pl.pallas_call(
        finish_kernel,
        name="finish",
        compiler_params=pltpu.CompilerParams(vmem_limit_bytes=2 * MEBI),
        out_shape=jax.ShapeDtypeStruct(residual.shape, jnp.float32),
        in_specs=[pl.BlockSpec(memory_space=pltpu.VMEM)] * 2,
        out_specs=pl.BlockSpec(memory_space=pltpu.VMEM),
    )(got, residual)


def body(queries, slot_key_cache, slot_value_cache, lengths, output_weight_matrix, residual):
    shards = lax.axis_size(SEQ)
    rows = queries.shape[0]
    sent, matrix = attend(
        lengths,
        queries[:, 0],
        slot_key_cache[:, 0],
        slot_value_cache[:, 0],
        output_weight_matrix[0, 0],
        shards,
    )
    lines, size = sent.shape
    got = lax.all_to_all(sent.reshape(lines, 1, size), SEQ, 0, 0, tiled=True).reshape(lines, size)
    sizes = [lax.axis_size(axis) for axis in MESH_AXES]
    chips = peer_chips(*sizes[:3])
    groups = [
        [(((x * sizes[1] + z) * sizes[2] + y) * sizes[3] + core) * sizes[4] + rep for x, z, y in chips]
        for core in range(sizes[3])
        for rep in range(sizes[4])
    ]
    places = [
        chips.index((x, z, y))
        for x in range(sizes[0])
        for z in range(sizes[1])
        for y in range(sizes[2])
    ]
    pieces = project(got, matrix, places, rows)
    both = lax.all_gather(pieces, "core")
    packed = core_sum(both)
    last = lax.all_to_all(packed, MESH_AXES, 0, 0, axis_index_groups=groups, tiled=True)
    return finish(last, residual)


def solution(mesh):
    fine = Mesh(
        mesh.devices.reshape(4, mesh.shape["seq"] // 4, mesh.shape["kvh"] // 2, 2, mesh.shape["rep"]),
        MESH_AXES,
    )
    in_specs = (
        P("rep", KVH, None, None),
        P("rep", KVH, SEQ, None),
        P("rep", KVH, SEQ, None),
        P("rep"),
        P(KVH, SEQ, None, None),
        P("rep", SEQ + KVH),
    )
    out_specs = P("rep", SEQ + KVH)
    return jax.shard_map(body, mesh=fine, in_specs=in_specs, out_specs=out_specs, check_vma=False)
```

```python
import math

import jax
import jax.numpy as jnp
from jax import lax
from jax.experimental import pallas as pl
from jax.experimental.pallas import tpu as pltpu
from jax.sharding import Mesh, PartitionSpec as P

BLOCK_POSITIONS = 32
LANES = 128
MEBI = 1 << 20
SEQ = ("x", "z_hi")
KVH = ("y", "core")
MESH_AXES = ("x", "z_hi", "y", "core", "rep")


def peer_chips(x_size, z_size, y_size):
    order = (0, 1, 3, 2)
    planes = (0, 2, 1, 3)
    chips = [
        (order[2 * x1 + x0], planes[z], order[2 * y1 + y0])
        for z in range(4)
        for x1 in range(2)
        for y1 in range(2)
        for x0 in range(2)
        for y0 in range(2)
    ]
    assert (x_size, z_size, y_size) == (4, 4, 4)
    return chips


def attend_kernel(shards, lengths_hbm, query_hbm, key_hbm, value_hbm, matrix_hbm, sent_ref, matrix_ref,
                  lengths_ref, query_ref, key_ref, value_ref, sems):
    rows, groups, size = query_ref.shape
    slots = key_ref.shape[1]
    lengths_copy, query_copy, key_copy, value_copy, matrix_copy = [
        pltpu.make_async_copy(source, target, sems.at[i])
        for i, (source, target) in enumerate(
            (
                (lengths_hbm, lengths_ref),
                (query_hbm, query_ref),
                (key_hbm, key_ref),
                (value_hbm, value_ref),
                (matrix_hbm, matrix_ref),
            )
        )
    ]
    lengths_copy.start()
    query_copy.start()
    key_copy.start()
    value_copy.start()
    matrix_copy.start()
    scale = 1.0 / math.sqrt(size)
    slot_ids = lax.broadcasted_iota(jnp.int32, (groups, slots), 1)
    positions = (
        slot_ids // BLOCK_POSITIONS * shards + lax.axis_index(SEQ)
    ) * BLOCK_POSITIONS + slot_ids % BLOCK_POSITIONS
    lane = lax.broadcasted_iota(jnp.int32, (groups, LANES), 1)
    lengths_copy.wait()
    query_copy.wait()
    key_copy.wait()
    scores = [
        lax.dot_general(
            query_ref[b], key_ref[b], (((1,), (1,)), ((), ())), preferred_element_type=jnp.float32
        )
        for b in range(rows)
    ]
    logs = jnp.zeros((groups, LANES), jnp.float32)
    weights = []
    totals = []
    for b in range(rows):
        masked = jnp.where(positions < lengths_ref[b], scores[b] * scale, -1e30)
        top = jnp.max(masked, axis=1, keepdims=True)
        weight = jnp.exp(masked - top)
        total = jnp.sum(weight, axis=1, keepdims=True)
        weights.append(weight.astype(jnp.bfloat16))
        totals.append(total)
        logs = jnp.where(lane == b, top + jnp.log(total), logs)
    value_copy.wait()
    for b in range(rows):
        summed = jnp.dot(weights[b], value_ref[b], preferred_element_type=jnp.float32)
        sent_ref[pl.ds(b, groups, stride=rows + 1), :] = summed / totals[b]
    sent_ref[pl.ds(rows, groups, stride=rows + 1), :] = logs
    matrix_copy.wait()


def attend(lengths, queries, keys, values, matrix, shards):
    rows, groups, size = queries.shape
    outside = pl.BlockSpec(memory_space=pltpu.HBM)
    inside = pl.BlockSpec(memory_space=pltpu.VMEM)
    operands = (lengths, queries, keys, values, matrix)
    return pl.pallas_call(
        lambda *refs: attend_kernel(shards, *refs),
        name="attend",
        compiler_params=pltpu.CompilerParams(vmem_limit_bytes=8 * MEBI),
        out_shape=(
            jax.ShapeDtypeStruct((groups * (rows + 1), size), jnp.float32),
            jax.ShapeDtypeStruct(matrix.shape, matrix.dtype),
        ),
        in_specs=[outside] * len(operands),
        out_specs=(inside, inside),
        scratch_shapes=[pltpu.SMEM(lengths.shape, lengths.dtype)]
        + [pltpu.VMEM(a.shape, a.dtype) for a in (queries, keys, values)]
        + [pltpu.SemaphoreType.DMA((len(operands),))],
    )(*[pltpu.with_memory_space_constraint(a, pltpu.HBM) for a in operands])


def project_kernel(places, got_ref, weight_ref, kept_ref, given_ref):
    pieces, part, lanes = kept_ref.shape
    rows = 2 * part
    half = lanes // 2
    shards = got_ref.shape[0] // (rows + 1)
    logs = got_ref[pl.ds(rows, shards, stride=rows + 1), :]
    factors = jnp.exp(logs - jnp.max(logs, axis=0, keepdims=True))
    factors = factors / jnp.sum(factors, axis=0, keepdims=True)
    lane = lax.broadcasted_iota(jnp.int32, (rows, lanes), 1)
    diagonal = lax.broadcasted_iota(jnp.int32, (rows, lanes), 0) == lane
    attended = jnp.zeros((rows, lanes), jnp.float32)
    for s in range(shards):
        factor = jnp.sum(
            jnp.where(diagonal, factors[s : s + 1, :], 0.0), axis=1, keepdims=True
        )
        attended += factor * got_ref[pl.ds(s * (rows + 1), rows), :]
    attended = attended.astype(jnp.bfloat16)
    low = lane[:part] < half
    first = lax.axis_index("core") == 0
    step = 8
    for start in range(0, pieces, step):
        product = jnp.dot(
            attended,
            weight_ref[:, start * lanes : (start + step) * lanes],
            preferred_element_type=jnp.float32,
        )
        for j in range(step):
            piece = product[:, j * lanes : (j + 1) * lanes]
            turned = pltpu.roll(piece, half, 1)
            zero = jnp.where(low, piece[:part], turned[part:])
            one = jnp.where(low, turned[:part], piece[part:])
            place = places[start + j]
            kept_ref[place] = jnp.where(first, zero, one)
            given_ref[place] = jnp.where(first, one, zero)


def project(got, weights, places, rows):
    size, features = weights.shape
    inside = pl.BlockSpec(memory_space=pltpu.VMEM)
    shape = jax.ShapeDtypeStruct((features // LANES, rows // 2, LANES), jnp.float32)
    return pl.pallas_call(
        lambda *refs: project_kernel(places, *refs),
        name="project",
        compiler_params=pltpu.CompilerParams(vmem_limit_bytes=8 * MEBI),
        out_shape=(shape, shape),
        in_specs=[inside, inside],
        out_specs=(inside, inside),
    )(got, weights)


def core_sum_kernel(kept_ref, both_ref, out_ref):
    first = lax.axis_index("core") == 0
    for i in range(out_ref.shape[0]):
        out_ref[i] = kept_ref[i] + jnp.where(first, both_ref[1, i], both_ref[0, i])


def core_sum(kept, both):
    inside = pl.BlockSpec(memory_space=pltpu.VMEM)
    return pl.pallas_call(
        core_sum_kernel,
        name="core_sum",
        compiler_params=pltpu.CompilerParams(vmem_limit_bytes=2 * MEBI),
        out_shape=jax.ShapeDtypeStruct(kept.shape, kept.dtype),
        in_specs=[inside, inside],
        out_specs=inside,
    )(kept, both)


def finish_kernel(got_ref, residual_ref, out_ref):
    width = out_ref.shape[1]
    part = got_ref.shape[1]
    totals = [got_ref[s] for s in range(got_ref.shape[0])]
    while len(totals) > 1:
        totals = [totals[i] + totals[i + 1] for i in range(0, len(totals), 2)]
    out_ref[:part] = residual_ref[:part] + totals[0][:, :width]
    out_ref[part:] = residual_ref[part:] + totals[0][:, width:]


def finish(got, residual):
    return pl.pallas_call(
        finish_kernel,
        name="finish",
        compiler_params=pltpu.CompilerParams(vmem_limit_bytes=2 * MEBI),
        out_shape=jax.ShapeDtypeStruct(residual.shape, jnp.float32),
        in_specs=[pl.BlockSpec(memory_space=pltpu.VMEM)] * 2,
        out_specs=pl.BlockSpec(memory_space=pltpu.VMEM),
    )(got, residual)


def body(queries, slot_key_cache, slot_value_cache, lengths, output_weight_matrix, residual):
    shards = lax.axis_size(SEQ)
    rows = queries.shape[0]
    sent, matrix = attend(
        lengths,
        queries[:, 0],
        slot_key_cache[:, 0],
        slot_value_cache[:, 0],
        output_weight_matrix[0, 0],
        shards,
    )
    lines, size = sent.shape
    got = lax.all_to_all(sent.reshape(lines, 1, size), SEQ, 0, 0, tiled=True).reshape(lines, size)
    sizes = [lax.axis_size(axis) for axis in MESH_AXES]
    chips = peer_chips(*sizes[:3])
    groups = [
        [(((x * sizes[1] + z) * sizes[2] + y) * sizes[3] + core) * sizes[4] + rep for x, z, y in chips]
        for core in range(sizes[3])
        for rep in range(sizes[4])
    ]
    places = [
        chips.index((x, z, y))
        for x in range(sizes[0])
        for z in range(sizes[1])
        for y in range(sizes[2])
    ]
    kept, given = project(got, matrix, places, rows)
    packed = core_sum(kept, lax.all_gather(given, "core"))
    last = lax.all_to_all(packed, MESH_AXES, 0, 0, axis_index_groups=groups, tiled=True)
    return finish(last, residual)


def solution(mesh):
    fine = Mesh(
        mesh.devices.reshape(4, mesh.shape["seq"] // 4, mesh.shape["kvh"] // 2, 2, mesh.shape["rep"]),
        MESH_AXES,
    )
    in_specs = (
        P("rep", KVH, None, None),
        P("rep", KVH, SEQ, None),
        P("rep", KVH, SEQ, None),
        P("rep"),
        P(KVH, SEQ, None, None),
        P("rep", SEQ + KVH),
    )
    out_specs = P("rep", SEQ + KVH)
    return jax.shard_map(body, mesh=fine, in_specs=in_specs, out_specs=out_specs, check_vma=False)
```

```python
import math

import jax
import jax.numpy as jnp
from jax import lax
from jax.experimental import pallas as pl
from jax.experimental.pallas import tpu as pltpu
from jax.sharding import Mesh, PartitionSpec as P

BLOCK_POSITIONS = 32
LANES = 128
MEBI = 1 << 20
SEQ = ("x", "z_hi")
KVH = ("y", "core")
MESH_AXES = ("x", "z_hi", "y", "core", "rep")


def peer_chips(x_size, z_size, y_size):
    order = (0, 1, 3, 2)
    planes = (0, 2, 1, 3)
    chips = [
        (order[2 * x1 + x0], planes[z], order[2 * y1 + y0])
        for z in range(4)
        for x1 in range(2)
        for y1 in range(2)
        for x0 in range(2)
        for y0 in range(2)
    ]
    assert (x_size, z_size, y_size) == (4, 4, 4)
    return chips


def attend_kernel(shards, lengths_hbm, query_hbm, key_hbm, value_hbm, matrix_hbm, sent_ref, matrix_ref,
                  lengths_ref, query_ref, key_ref, value_ref, sems):
    rows, groups, size = query_ref.shape
    slots = key_ref.shape[1]
    lengths_copy, query_copy, key_copy, value_copy, matrix_copy = [
        pltpu.make_async_copy(source, target, sems.at[i])
        for i, (source, target) in enumerate(
            (
                (lengths_hbm, lengths_ref),
                (query_hbm, query_ref),
                (key_hbm, key_ref),
                (value_hbm, value_ref),
                (matrix_hbm, matrix_ref),
            )
        )
    ]
    lengths_copy.start()
    query_copy.start()
    key_copy.start()
    value_copy.start()
    matrix_copy.start()
    scale = 1.0 / math.sqrt(size)
    slot_ids = lax.broadcasted_iota(jnp.int32, (groups, slots), 1)
    positions = (
        slot_ids // BLOCK_POSITIONS * shards + lax.axis_index(SEQ)
    ) * BLOCK_POSITIONS + slot_ids % BLOCK_POSITIONS
    lane = lax.broadcasted_iota(jnp.int32, (groups, LANES), 1)
    lengths_copy.wait()
    query_copy.wait()
    key_copy.wait()
    scores = [
        lax.dot_general(
            query_ref[b], key_ref[b], (((1,), (1,)), ((), ())), preferred_element_type=jnp.float32
        )
        for b in range(rows)
    ]
    logs = jnp.zeros((groups, LANES), jnp.float32)
    weights = []
    totals = []
    for b in range(rows):
        masked = jnp.where(positions < lengths_ref[b], scores[b] * scale, -1e30)
        top = jnp.max(masked, axis=1, keepdims=True)
        weight = jnp.exp(masked - top)
        total = jnp.sum(weight, axis=1, keepdims=True)
        weights.append(weight.astype(jnp.bfloat16))
        totals.append(total)
        logs = jnp.where(lane == b, top + jnp.log(total), logs)
    value_copy.wait()
    for b in range(rows):
        summed = jnp.dot(weights[b], value_ref[b], preferred_element_type=jnp.float32)
        sent_ref[pl.ds(b, groups, stride=rows + 1), :] = summed / totals[b]
    sent_ref[pl.ds(rows, groups, stride=rows + 1), :] = logs
    matrix_copy.wait()


def attend(lengths, queries, keys, values, matrix, shards):
    rows, groups, size = queries.shape
    outside = pl.BlockSpec(memory_space=pltpu.HBM)
    inside = pl.BlockSpec(memory_space=pltpu.VMEM)
    operands = (lengths, queries, keys, values, matrix)
    return pl.pallas_call(
        lambda *refs: attend_kernel(shards, *refs),
        name="attend",
        compiler_params=pltpu.CompilerParams(vmem_limit_bytes=8 * MEBI),
        out_shape=(
            jax.ShapeDtypeStruct((groups * (rows + 1), size), jnp.float32),
            jax.ShapeDtypeStruct(matrix.shape, matrix.dtype),
        ),
        in_specs=[outside] * len(operands),
        out_specs=(inside, inside),
        scratch_shapes=[pltpu.SMEM(lengths.shape, lengths.dtype)]
        + [pltpu.VMEM(a.shape, a.dtype) for a in (queries, keys, values)]
        + [pltpu.SemaphoreType.DMA((len(operands),))],
    )(*[pltpu.with_memory_space_constraint(a, pltpu.HBM) for a in operands])


def project_kernel(places, got_ref, weight_ref, out_ref):
    pieces, rows, lanes = out_ref.shape
    shards = got_ref.shape[0] // (rows + 1)
    logs = got_ref[pl.ds(rows, shards, stride=rows + 1), :]
    factors = jnp.exp(logs - jnp.max(logs, axis=0, keepdims=True))
    factors = factors / jnp.sum(factors, axis=0, keepdims=True)
    diagonal = lax.broadcasted_iota(jnp.int32, (rows, lanes), 0) == lax.broadcasted_iota(
        jnp.int32, (rows, lanes), 1
    )
    attended = jnp.zeros((rows, lanes), jnp.float32)
    for s in range(shards):
        factor = jnp.sum(
            jnp.where(diagonal, factors[s : s + 1, :], 0.0), axis=1, keepdims=True
        )
        attended += factor * got_ref[pl.ds(s * (rows + 1), rows), :]
    attended = attended.astype(jnp.bfloat16)
    step = 32
    for first in range(0, pieces, step):
        product = jnp.dot(
            attended,
            weight_ref[:, first * lanes : (first + step) * lanes],
            preferred_element_type=jnp.float32,
        )
        for j in range(step):
            out_ref[places[first + j]] = product[:, j * lanes : (j + 1) * lanes]


def project(got, weights, places, rows):
    size, features = weights.shape
    return pl.pallas_call(
        lambda *refs: project_kernel(places, *refs),
        name="project",
        compiler_params=pltpu.CompilerParams(vmem_limit_bytes=8 * MEBI),
        out_shape=jax.ShapeDtypeStruct((features // LANES, rows, LANES), jnp.float32),
        in_specs=[pl.BlockSpec(memory_space=pltpu.VMEM)] * 2,
        out_specs=pl.BlockSpec(memory_space=pltpu.VMEM),
    )(got, weights)


def core_sum_kernel(got_ref, out_ref):
    pieces, part, lanes = out_ref.shape
    half = lanes // 2
    low = lax.broadcasted_iota(jnp.int32, (part, lanes), 1) < half
    first = lax.axis_index("core") == 0
    for i in range(pieces):
        total = got_ref[0, i] + got_ref[1, i]
        other = pltpu.roll(total, half, 1)
        one = jnp.where(first, total, other)
        two = jnp.where(first, other, total)
        out_ref[i] = jnp.where(low, one[:part], two[part:])


def core_sum(got):
    cores, pieces, rows, lanes = got.shape
    return pl.pallas_call(
        core_sum_kernel,
        name="core_sum",
        compiler_params=pltpu.CompilerParams(vmem_limit_bytes=2 * MEBI),
        out_shape=jax.ShapeDtypeStruct((pieces, rows // cores, lanes), jnp.float32),
        in_specs=[pl.BlockSpec(memory_space=pltpu.VMEM)],
        out_specs=pl.BlockSpec(memory_space=pltpu.VMEM),
    )(got)


def finish_kernel(got_ref, residual_ref, out_ref):
    width = out_ref.shape[1]
    part = got_ref.shape[1]
    totals = [got_ref[s] for s in range(got_ref.shape[0])]
    while len(totals) > 1:
        totals = [totals[i] + totals[i + 1] for i in range(0, len(totals), 2)]
    out_ref[:part] = residual_ref[:part] + totals[0][:, :width]
    out_ref[part:] = residual_ref[part:] + totals[0][:, width:]


def finish(got, residual):
    return pl.pallas_call(
        finish_kernel,
        name="finish",
        compiler_params=pltpu.CompilerParams(vmem_limit_bytes=2 * MEBI),
        out_shape=jax.ShapeDtypeStruct(residual.shape, jnp.float32),
        in_specs=[pl.BlockSpec(memory_space=pltpu.VMEM)] * 2,
        out_specs=pl.BlockSpec(memory_space=pltpu.VMEM),
    )(got, residual)


def body(queries, slot_key_cache, slot_value_cache, lengths, output_weight_matrix, residual):
    shards = lax.axis_size(SEQ)
    rows = queries.shape[0]
    sent, matrix = attend(
        lengths,
        queries[:, 0],
        slot_key_cache[:, 0],
        slot_value_cache[:, 0],
        output_weight_matrix[0, 0],
        shards,
    )
    lines, size = sent.shape
    got = lax.all_to_all(sent.reshape(lines, 1, size), SEQ, 0, 0, tiled=True).reshape(lines, size)
    sizes = [lax.axis_size(axis) for axis in MESH_AXES]
    chips = peer_chips(*sizes[:3])
    groups = [
        [(((x * sizes[1] + z) * sizes[2] + y) * sizes[3] + core) * sizes[4] + rep for x, z, y in chips]
        for core in range(sizes[3])
        for rep in range(sizes[4])
    ]
    places = [
        chips.index((x, z, y))
        for x in range(sizes[0])
        for z in range(sizes[1])
        for y in range(sizes[2])
    ]
    pieces = project(got, matrix, places, rows)
    both = lax.all_gather(pieces, "core")
    packed = core_sum(both)
    last = lax.all_to_all(packed, MESH_AXES, 0, 0, axis_index_groups=groups, tiled=True)
    return finish(last, residual)


def solution(mesh):
    fine = Mesh(
        mesh.devices.reshape(4, mesh.shape["seq"] // 4, mesh.shape["kvh"] // 2, 2, mesh.shape["rep"]),
        MESH_AXES,
    )
    in_specs = (
        P("rep", KVH, None, None),
        P("rep", KVH, SEQ, None),
        P("rep", KVH, SEQ, None),
        P("rep"),
        P(KVH, SEQ, None, None),
        P("rep", SEQ + KVH),
    )
    out_specs = P("rep", SEQ + KVH)
    return jax.shard_map(body, mesh=fine, in_specs=in_specs, out_specs=out_specs, check_vma=False)
```
